256 devices in a mesh: wide: 32 (over x, z), narrow: 8 (over y, core).
Axes of the slice: x: 4, y: 4, z: 8, core: 2. Of those that a mesh axis runs over, the one named last changes fastest.
Arguments:
- hidden_in: bfloat16 [16384, 1664], P(('wide', 'narrow')), may hold values from -3 to 3
- queries: bfloat16 [16, 1024, 1664], P('narrow', 'wide'), may hold values from -24 to 24
- keys: bfloat16 [16, 1024, 1664], P('narrow', 'wide'), may hold values from -24 to 24
- values: bfloat16 [16, 1024, 1664], P('narrow', 'wide'), may hold values from -12 to 12
- out_weight: bfloat16 [1664, 1664], P('narrow', 'wide'), may hold values from -0.25 to 0.25
- merge_weight: bfloat16 [4, 1664, 1664], P(None, 'narrow', 'wide'), may hold values from -0.125 to 0.125
- segment_ids: int32 [4096], P('wide'), may hold values from 0 to 15, never falling along the last dimension, each value on 1 to 2560 neighbouring positions
- owners: int32 [4096, 1], P('wide'), may hold values from 0 to 31; in each aligned block of 128 rows (0 to 127, 128 to 255, ...) at most 8 rows name the same one
Outputs:
- hidden_out: bfloat16 [16384, 1664], P(('wide', 'narrow'))
- delivered: bfloat16 [8192, 1664], P('wide', 'narrow')
The draws below stay inside these ranges and needn't reach their ends.
Inputs may be any that keep to these rules, and one draw needn't show every extreme that they name: `segment_ids`: never falling along the tokens; the largest image or clip holds exactly 2560 merged tokens. `owners`: among the merged tokens of one index of wide, at most 8 share an owner, and exactly 8 do for some owner.
All inputs are finite; a program needn't handle non-finite values.
Results may differ from the reference program's by a relative error of at most 0.025.
Values may be sent and summed in bfloat16 or wider, within the bound.
A program may use at most 64 MiB of HBM per device.

```python
import math
import jax
import jax.numpy as jnp
import numpy as np
from jax import lax

D = 1664
HEADS = 16
HEAD_DIM = 104
DOUT = 1664
TOKENS = 16384
MERGED_DEV = 128
MERGED = 4096
CAP = 8
SLOTS = 256
SEGS = 16
LONGEST = 2560
N_WIDE = 32


def drawn_field(key, salt):
    return jnp.clip(1.41 * jax.random.normal(jax.random.fold_in(key, salt), (TOKENS, D), jnp.float32), -8.5, 8.5)


def head_layout(field):
    return field.reshape(TOKENS, HEADS, HEAD_DIM).transpose(1, 0, 2).reshape(HEADS, TOKENS // 16, 16 * HEAD_DIM)


def draw_queries(key, part):
    field = drawn_field(key, 11)
    return head_layout(field).astype(jnp.bfloat16)


def draw_keys(key, part):
    field = drawn_field(key, 13)
    return head_layout(field).astype(jnp.bfloat16)


def strengthened(values, stream_key, source, target, parts, factor):
    def block_of(position):
        return (jnp.arange(values.shape[position]) // (values.shape[position] // parts)).reshape((-1,) + (1,) * (values.ndim - 1 - position))

    near = jax.random.permutation(stream_key, parts)[block_of(target)]
    other_side = (block_of(target) + parts // 2) % parts
    return jnp.where((block_of(source) == near) | (block_of(source) == other_side), factor * values, values)


def levels(stream_key, shape, shards, least, high):
    def one(dim, blocks):
        draws = jax.random.uniform(jax.random.fold_in(jax.random.fold_in(stream_key, 6), dim), (blocks,), jnp.float32, least / len(shards), high / len(shards))
        return jnp.repeat(jnp.exp(draws), shape[dim] // blocks).reshape((-1,) + (1,) * (len(shape) - dim - 1))

    factor_of = one(*shards[0])
    for cut in shards[1:]:
        factor_of = factor_of * one(*cut)
    return factor_of


def profile(amount, total, reach, lean):
    weights = [(1 << 20) // math.isqrt(standing ** lean) + 1 for standing in range(2, amount + 1)]
    rest, counts = total - reach - (amount - 1), [1] * (amount - 1)
    while rest > 0:
        movable = [i for i in range(amount - 1) if counts[i] < reach]
        pool, remaining = sum([weights[i] for i in movable]), rest
        for i in movable:
            addition = min(reach - counts[i], max(1, remaining * weights[i] // pool), rest)
            counts[i] = counts[i] + addition
            rest = rest - addition
    return np.array([reach] + counts)


def uneven_parts(own_key, count, total, most, slope):
    if count == 2:
        one = jax.random.randint(own_key, (), max(1, total - most), min(most, total - 1) + 1)
        return jnp.stack([one, total - one])
    tallies = jnp.asarray(profile(count, total, most, slope), jnp.int32)
    twos = (count - 1) // 2
    giver, receiver = tallies[1:1 + 2 * twos:2], tallies[2:2 + 2 * twos:2]
    room = jnp.minimum(giver - 1, most - receiver)
    shifted = jax.random.randint(jax.random.fold_in(own_key, 1), (twos,), 0, 1 << 20) % (room + 1)
    tallies = tallies.at[1:1 + 2 * twos:2].set(giver - shifted).at[2:2 + 2 * twos:2].set(receiver + shifted)
    return tallies[jax.random.permutation(jax.random.fold_in(own_key, 2), count)]


def deal_out(stream_key, own, number, rows, number_of, top, most, lean):
    sequence = jax.random.permutation(stream_key, number_of)
    packed, common = portions_of(number_of, rows * top, most, lean, True), portions_of(number_of, rows * top, most, lean, False)
    places = jnp.arange(number_of)

    def named(lengths, rotation):
        used = int((lengths > 0).sum())
        fixed = max(1, used // 4)
        passed = fixed + (places - fixed + rotation * (used - fixed)) % max(1, number_of - fixed)
        return jnp.zeros((number_of,), jnp.int32).at[sequence[jnp.where(places < fixed, places, passed)]].set(jnp.asarray(lengths, jnp.int32))

    lengths = jnp.where(number % 4 == 0, named(packed, number // 4), named(common, number - number // 4 - 1))
    mixed = jax.random.permutation(jax.random.fold_in(own, 3), number_of)
    giver, receiver = mixed[0:number_of // 2 * 2:2], mixed[1:number_of // 2 * 2:2]
    margin = jnp.minimum(lengths[giver] - 1, most - lengths[receiver]) // 2
    margin = jnp.where((giver == sequence[0]) | (receiver == sequence[0]) | (lengths[receiver] == 0), 0, jnp.maximum(margin, 0))
    passed = jax.random.randint(jax.random.fold_in(own, 4), (number_of // 2,), 0, 1 << 20) % (margin + 1)
    lengths = lengths.at[giver].add(-passed).at[receiver].add(passed)
    members = jnp.searchsorted(jnp.cumsum(lengths), jnp.arange(rows * top), side="right").astype(jnp.int32)
    grid = members.reshape(top, rows).T
    grid = grid[jax.random.permutation(jax.random.fold_in(own, 1), rows)]
    rotation = jax.random.randint(jax.random.fold_in(own, 2), (rows, 1), 0, top)
    return jnp.take_along_axis(grid, (jnp.arange(top)[None, :] + rotation) % top, axis=1)


def portions_of(count, total, bound, lean, full):
    loads = [(1 << 20) // math.isqrt(standing ** lean) + 1 for standing in range(1, count + 1)]
    largest = bound if full else min(bound, max(-(-total // count), total * loads[0] // sum(loads)))
    least = 1 if total - largest >= count - 1 else 0
    holding, spare = [largest] + [least] * (count - 1), total - largest - least * (count - 1)
    while spare > 0:
        free = [i for i in range(1, count) if holding[i] < largest] or [i for i in range(1, count) if holding[i] < bound]
        pool, left = sum([loads[i] for i in free]), spare
        for i in free:
            more = min(bound - holding[i], max(1, left * loads[i] // pool), spare)
            holding[i] = holding[i] + more
            spare = spare - more
    return np.array(holding)


def centred(stream_key, dims, scale, limit, pieces=(), kind=jnp.bfloat16):
    entries = scale * jax.random.normal(stream_key, dims, jnp.float32)
    if pieces:
        entries = entries * levels(stream_key, dims, pieces, -0.22, 0.18)
    return jnp.clip(entries, -limit, limit).astype(kind)


def noise_with(own_key, extent, scale, reach, pieces, heavy, kind=jnp.bfloat16):
    entries = scale * jax.random.normal(own_key, extent, jnp.float32)
    if pieces:
        entries = entries * levels(own_key, extent, pieces, -0.22, 0.18)
    return jnp.clip(strengthened(entries, jax.random.fold_in(own_key, 3), *heavy), -reach, reach).astype(kind)


def setup_inputs(seed: int = 0) -> dict:
    key_of = jax.random.split(jax.random.key(seed), 9)
    hidden_in = centred(key_of[0], (TOKENS, D), 0.5, 3.0, ((0, 256),))
    queries = draw_queries(jax.random.fold_in(key_of[8], 71), 0)
    keys = draw_keys(jax.random.fold_in(key_of[8], 71), 0)
    values = centred(key_of[3], (HEADS, TOKENS // 16, 16 * HEAD_DIM), 2.0, 12.0, ((0, 8), (1, 32)))
    out_weight = noise_with(key_of[4], (D, D), D ** -0.5, 0.25, ((0, 8), (1, 32)), (0, 1, 32, 2.75))
    merge_weight = noise_with(key_of[5], (4, D, DOUT), (4 * D) ** -0.5, 0.125, ((1, 8), (2, 32)), (1, 2, 32, 2.75))
    segment_ids = jnp.searchsorted(jnp.cumsum(uneven_parts(key_of[6], SEGS, MERGED, LONGEST, 2)), jnp.arange(MERGED), side="right").astype(jnp.int32)
    owners_keys = jax.random.split(jax.random.fold_in(key_of[7], 1), MERGED // MERGED_DEV)
    owners_turns = jax.random.permutation(jax.random.fold_in(key_of[7], 3), MERGED // MERGED_DEV)
    owners = jax.vmap(lambda own, number: deal_out(jax.random.fold_in(key_of[7], 2), own, number, MERGED_DEV, N_WIDE, 1, CAP, 2))(owners_keys, owners_turns).reshape((MERGED, 1))
    return {"hidden_in": hidden_in, "queries": queries, "keys": keys, "values": values, "out_weight": out_weight, "merge_weight": merge_weight, "segment_ids": segment_ids, "owners": owners}


NEG = -1e+30

def reference(hidden_in, queries, keys, values, out_weight, merge_weight, segment_ids, owners):
    tok_seg = jnp.repeat(segment_ids, 4)
    scale = 1.0 / math.sqrt(HEAD_DIM)
    q_heads = queries.reshape(HEADS, TOKENS, HEAD_DIM)
    k_heads = keys.reshape(HEADS, TOKENS, HEAD_DIM)
    v_heads = values.reshape(HEADS, TOKENS, HEAD_DIM)
    q_block = min(512, TOKENS)
    n_blocks = TOKENS // q_block

    def per_head(operands):
        q_all, k_all, v_all = operands

        def per_block(pair):
            q_rows, s_rows = pair
            scores = jnp.dot(q_rows, k_all.T, preferred_element_type=jnp.float32) * scale
            keep = s_rows[:, None] == tok_seg[None, :]
            scores = jnp.where(keep, scores, NEG)
            top = lax.optimization_barrier(jnp.max(scores, axis=-1, keepdims=True))
            weights = jnp.where(keep, jnp.exp(scores - top), 0.0)
            total = lax.optimization_barrier(jnp.sum(weights, axis=-1, keepdims=True))
            return jnp.dot(weights.astype(jnp.bfloat16), v_all, preferred_element_type=jnp.float32) / total
        return lax.map(per_block, (q_all.reshape(n_blocks, q_block, HEAD_DIM), tok_seg.reshape(n_blocks, q_block)))
    result = lax.map(per_head, (q_heads, k_heads, v_heads))
    attn = result.reshape(HEADS, TOKENS, HEAD_DIM).transpose(1, 0, 2).reshape(TOKENS, D).astype(jnp.bfloat16)
    mix = jnp.dot(attn, out_weight, preferred_element_type=jnp.float32)
    hidden_out = (hidden_in.astype(jnp.float32) + mix).astype(jnp.bfloat16)
    merged = hidden_out.reshape(MERGED, 4 * D)
    feature = jnp.dot(merged, merge_weight.reshape(4 * D, DOUT), preferred_element_type=jnp.float32).astype(jnp.bfloat16)
    owner_blocks = owners[:, 0].reshape(N_WIDE, MERGED_DEV)
    onehot = (owner_blocks[:, :, None] == jnp.arange(N_WIDE, dtype=jnp.int32)[None, None, :]).astype(jnp.int32)
    rank = lax.optimization_barrier(jnp.sum(jnp.cumsum(onehot, axis=1) * onehot, axis=2)) - 1
    source = jnp.broadcast_to(jnp.arange(N_WIDE, dtype=jnp.int32)[:, None], (N_WIDE, MERGED_DEV))
    table = jnp.zeros((N_WIDE, N_WIDE, CAP, DOUT), feature.dtype)
    table = table.at[owner_blocks, source, rank].set(feature.reshape(N_WIDE, MERGED_DEV, DOUT))
    return (hidden_out, table.reshape(N_WIDE * SLOTS, DOUT))
```

```python
import math

import jax
import jax.numpy as jnp
from jax import lax
from jax.experimental import pallas as pl
from jax.experimental.pallas import tpu as pltpu
from jax.sharding import PartitionSpec as P

HD = 104
X, Z, Y = 4, 8, 4
NW, NN = 32, 8
D = 1664
TILE = 2048
BIG = 2.0**100
bf16, f32, i32 = jnp.bfloat16, jnp.float32, jnp.int32
MESH = pl.DeviceIdType.MESH


def iota(shape, dim):
    return lax.broadcasted_iota(i32, shape, dim)


def kernel(q_ref, k_ref, v_ref, seg_ref, own_ref, hin_ref, wout_ref, wm_ref,
           hout_ref, dout_ref,
           kv, qb, oh, tr, kx, vx, qx, m_s, acc_s, ob, orecv, hb, hrecv, fb, frecv, outg, drecv,
           s0, r_kv, r_q, r_oh, ss, rs, dss, drs, so, ro, sh, rh, sf, rf, sd, rd):
    w = lax.axis_index("wide")
    n = lax.axis_index("narrow")
    x, z = w // Z, w % Z
    y, c = n // 2, n % 2
    up = 1 - 2 * c
    scale = math.log2(math.e) / math.sqrt(HD)

    def is_me(dw, dn):
        return (dw == w) & (dn == n)

    def remote(src, dst, ssem, rsem, dw, dn):
        return pltpu.make_async_remote_copy(src_ref=src, dst_ref=dst, send_sem=ssem, recv_sem=rsem,
                                            device_id=(dw, dn), device_id_type=MESH)

    def send(src, dst, ssem, rsem, dw, dn):
        @pl.when(jnp.logical_not(is_me(dw, dn)))
        def _():
            remote(src, dst, ssem, rsem, dw, dn).start()

        @pl.when(is_me(dw, dn))
        def _():
            pltpu.make_async_copy(src, dst, rsem).start()

    def sent(src, ssem, dw, dn):
        @pl.when(jnp.logical_not(is_me(dw, dn)))
        def _():
            remote(src, src, ssem, ssem, dw, dn).wait_send()

    def arrived(dst, rsem):
        remote(dst, dst, rsem, rsem, w, n).wait_recv()

    barrier = pltpu.get_barrier_semaphore()

    @pl.loop(0, X * NN)
    def _(i):
        dw, dn = (i // NN) * Z + z, i % NN

        @pl.when(jnp.logical_not(is_me(dw, dn)))
        def _():
            pl.semaphore_signal(barrier, inc=1, device_id=(dw, dn), device_id_type=MESH)

    @pl.loop(0, NW)
    def _(i):
        @pl.when(i % Z != z)
        def _():
            pl.semaphore_signal(barrier, inc=1, device_id=(i, n), device_id_type=MESH)

    t = (iota((128, 128), 0) == seg_ref[...] + 32 * (iota((1, 128), 1) & 3)).astype(f32)
    tr[...] = t.T
    oh[...] = (tr[pl.ds(0, 32, stride=4), :] + tr[pl.ds(1, 32, stride=4), :]
               + tr[pl.ds(2, 32, stride=4), :] + tr[pl.ds(3, 32, stride=4), :]).astype(bf16)

    g64, p64 = iota((64, 64), 0), iota((64, 64), 1)
    perm = (p64 == 4 * (g64 & 15) + (g64 >> 4)).astype(bf16)
    hp = jnp.dot(perm, hin_ref[...], preferred_element_type=f32).astype(bf16)
    hb[...] = jnp.zeros_like(hb)
    for i in range(NN):
        hb[i, :, 0:208] = hp[:, 208 * i:208 * i + 208]

    owner_row = own_ref[...]
    owner_col = jnp.broadcast_to(owner_row.astype(f32), (128, 128)).T
    same = (owner_col == owner_row.astype(f32)) & (iota((128, 128), 0) < iota((128, 128), 1))
    rank = jnp.sum(same.astype(f32), axis=0, keepdims=True)
    slot_of = owner_row * 8 + rank.astype(i32)
    picker = (iota((256, 128), 0) == slot_of).astype(bf16)

    pl.semaphore_wait(barrier, X * NN - 1 + NW - X)

    rows_x = pl.ds(pl.multiple_of(32 * x, 32), 32)
    rows_q = pl.ds(pl.multiple_of(16 * x, 16), 16)
    main, tail = pl.ds(0, D), pl.ds(D, 128)
    starts = []
    for i in range(2):
        dw = (2 * c + i) * Z + z
        starts.append((k_ref.at[i], kv.at[0, z, rows_x, main], s0.at[i], r_kv.at[x], dw, 2 * y))
        starts.append((v_ref.at[i], kv.at[1, z, rows_x, main], s0.at[2 + i], r_kv.at[x], dw, 2 * y + 1))
    for i in range(2):
        dw = (2 * c + i) * Z + z
        for d in range(2):
            starts.append((q_ref.at[i, pl.ds(16 * d, 16)], qb.at[rows_q], s0.at[4 + 2 * i + d], r_q.at[x], dw,
                           2 * y + d))
    for dx in range(X):
        starts.append((oh, kv.at[c, z, rows_x, tail], s0.at[8 + dx], r_oh.at[x], dx * Z + z, n))
    for args in starts:
        send(*args)

    m_s[...] = jnp.full_like(m_s, -3e38)
    acc_s[...] = jnp.zeros_like(acc_s)

    lane = iota((128, 128), 1)
    ones_col = (lane == HD).astype(bf16)

    def piece(ref_slice, j):
        t, r = (HD * j) // 128, (HD * j) % 128
        out = ref_slice(t)
        if r:
            out = pltpu.roll(out, 128 - r, 1)
        if r + HD > 128:
            nxt = pltpu.roll(ref_slice(t + 1), 128 - r, 1)
            out = jnp.where(iota(out.shape, 1) < 128 - r, out, nxt)
        return out

    def attend(slot):
        ohs = kv[0, slot, :, D:D + 128]
        for jj in range(4):
            ohr = pltpu.roll(ohs, (HD - 32 * jj) % 128, 1)
            for j in range(4 * jj, 4 * jj + 4):
                kj = piece(lambda t: kv[0, slot, :, 128 * t:128 * t + 128], j)
                kx[128 * j:128 * j + 128, :] = jnp.where(lane < HD, kj, ohr)
                vj = piece(lambda t: kv[1, slot, :, 128 * t:128 * t + 128], j)
                vx[128 * j:128 * j + 128, :] = jnp.where(lane < HD, vj, ones_col)

        @pl.loop(0, X)
        def _(qt):
            rows = pl.ds(pl.multiple_of(256 * qt, 256), 256)
            s = lax.dot_general(qx[rows, :], kx[...], (((1,), (1,)), ((), ())), preferred_element_type=f32)
            m_old = m_s[rows, :]
            m_new = jnp.maximum(m_old, jnp.max(s, axis=1, keepdims=True))
            p = jnp.exp2((s - m_new) * scale).astype(bf16)
            fix = jnp.exp2((m_old - m_new) * scale)
            acc_s[rows, :] = acc_s[rows, :] * fix + jnp.dot(p, vx[...], preferred_element_type=f32)
            m_s[rows, :] = m_new

    for i in range(X):
        arrived(kv.at[c, z, pl.ds(32 * i, 32), main], r_kv.at[i])
        arrived(kv.at[c, z, pl.ds(32 * i, 32), tail], r_oh.at[i])

    def slot_at(k):
        h = (k + 1) // 2
        sign = jnp.where(k % 2 == 1, -1, 1)
        return (z + sign * up * h + 2 * Z) % Z

    def to_partner(slot):
        return remote(kv.at[c, slot], kv.at[c, slot], dss.at[slot], drs.at[slot], w, n + up)

    def onward(k, t):
        slot = slot_at(k)
        step = jnp.where(t % 2 == 1, up, -up)
        dz = (z + step + Z) % Z
        return remote(kv.at[c, slot], kv.at[c, slot], ss.at[t], rs.at[t], x * Z + dz, n)

    onward(0, 1).start()
    onward(0, 2).start()
    to_partner(z).start()

    for i in range(X):
        arrived(qb.at[pl.ds(16 * i, 16)], r_q.at[i])
    lane16 = iota((16, 128), 1)
    for i in range(X):
        ohq = kv[c, z, pl.ds(pl.multiple_of(32 * i + 16 * c, 16), 16), D:D + 128]
        for jj in range(4):
            ohr = (pltpu.roll(ohq, (HD - 32 * jj) % 128, 1) - bf16(1)) * bf16(BIG)
            ohr = jnp.where(lane16 < HD + 16, ohr, bf16(0))
            for j in range(4 * jj, 4 * jj + 4):
                qj = piece(lambda t: qb[16 * i:16 * i + 16, 128 * t:128 * t + 128], j)
                qx[256 * i + 16 * j:256 * i + 16 * j + 16, :] = jnp.where(lane16 < HD, qj, ohr)

    @pl.loop(0, Z)
    def _(k):
        def take(kk):
            slot = slot_at(kk)
            arrived(kv.at[c, slot], rs.at[kk])

            @pl.when(kk + 2 < Z)
            def _():
                onward(kk, kk + 2).start()
            to_partner(slot).start()

        @pl.when(k % 2 == 1)
        def _():
            take(k)

            @pl.when(k + 1 < Z)
            def _():
                take(k + 1)
        slot = slot_at(k)
        arrived(kv.at[1 - c, slot], drs.at[slot])
        attend(slot)

    i0, i1 = iota((256, 256), 0), iota((256, 256), 1)
    grp, pos = i0 & 15, (i0 >> 4) & 3
    r_src = 4 * (i0 >> 6) + (grp >> 2)
    j_src = 4 * (grp & 3) + pos
    perm256 = (i1 == j_src * 16 + r_src).astype(bf16)
    lane256 = iota((256, 128), 1)
    for i in range(X):
        a = acc_s[256 * i:256 * i + 256, :]
        a = jnp.where(lane256 < HD, a / a[:, HD:HD + 1], 0.0).astype(bf16)
        ob[4 * i:4 * i + 4] = jnp.dot(perm256, a, preferred_element_type=f32).astype(bf16).reshape(4, 64, 128)
    head = 4 * y + x
    for i in range(X):
        for l in range(4):
            send(ob.at[4 * i + l], orecv.at[head], so.at[4 * i + l], ro.at[head], i * Z + z, 4 * c + l)

    hid = jnp.zeros((64, TILE), f32)
    for hp2 in range(8):
        arrived(orecv.at[2 * hp2], ro.at[2 * hp2])
        arrived(orecv.at[2 * hp2 + 1], ro.at[2 * hp2 + 1])
        a = jnp.concatenate([orecv[2 * hp2], orecv[2 * hp2 + 1]], axis=1)
        hid = hid + jnp.dot(a, wout_ref[256 * hp2:256 * hp2 + 256, :], preferred_element_type=f32)
    for i in range(NN):
        hb[i] = (hb[i].astype(f32) + hid[:, 256 * i:256 * i + 256]).astype(bf16)
    for i in range(NN):
        send(hb.at[i], hrecv.at[n], sh.at[i], rh.at[n], w, i)
    whole = jnp.concatenate([hb[i][:, 0:208] for i in range(NN)], axis=1)
    back = (g64 == 4 * (p64 & 15) + (p64 >> 4)).astype(bf16)
    hout_ref[...] = jnp.dot(back, whole, preferred_element_type=f32).astype(bf16)

    for i in range(NN):
        arrived(hrecv.at[i], rh.at[i])
    part = jnp.zeros((128, TILE), f32)
    for j in range(4):
        part = part + jnp.dot(hrecv[:, 16 * j:16 * j + 16, :].reshape(128, 256), wm_ref[j],
                              preferred_element_type=f32)
    for i in range(NN):
        fb[i] = part[:, 256 * i:256 * i + 256].astype(bf16)
    for i in range(NN):
        send(fb.at[i], frecv.at[n], sf.at[i], rf.at[n], w, i)
    feat = jnp.zeros((128, 256), f32)
    for i in range(NN):
        arrived(frecv.at[i], rf.at[i])
        feat = feat + frecv[i].astype(f32)

    outg[...] = jnp.dot(picker, feat.astype(bf16), preferred_element_type=f32).reshape(NW, 8, 256).astype(bf16)

    @pl.loop(0, NW)
    def _(i):
        send(outg.at[i], drecv.at[w], sd.at[i], rd.at[w], i, n)

    @pl.loop(0, NW)
    def _(i):
        arrived(drecv.at[i], rd.at[i])
    dout_ref[...] = drecv[...].astype(f32).reshape(256, 256).astype(bf16)[:, 0:208]

    for src, dst, ssem, rsem, dw, dn in starts:
        sent(src, ssem, dw, dn)

    @pl.loop(1, Z)
    def _(t):
        onward(jnp.maximum(t - 2, 0), t).wait_send()

    @pl.loop(0, Z)
    def _(t):
        to_partner(t).wait_send()
    for i in range(X):
        for l in range(4):
            sent(ob.at[4 * i + l], so.at[4 * i + l], i * Z + z, 4 * c + l)
    for i in range(NN):
        sent(hb.at[i], sh.at[i], w, i)
        sent(fb.at[i], sf.at[i], w, i)

    @pl.loop(0, NW)
    def _(i):
        sent(outg.at[i], sd.at[i], i, n)


def shards(hidden_in, queries, keys, values, out_weight, merge_weight, segment_ids, owners):
    wout = lax.all_gather(out_weight, "wide", axis=1, tiled=True)
    wout = lax.all_gather(wout, "narrow", axis=0, tiled=True)
    wout = jnp.pad(wout.reshape(16, HD, NN, 208), ((0, 0), (0, 24), (0, 0), (0, 48))).reshape(TILE, TILE)
    wm = lax.all_gather(merge_weight, "wide", axis=2, tiled=True)
    wm = jnp.pad(wm.reshape(4, 208, NN, 208), ((0, 0), (0, 48), (0, 0), (0, 48))).reshape(4, 256, TILE)
    vm = pl.BlockSpec(memory_space=pltpu.VMEM)
    dma = pltpu.SemaphoreType.DMA
    return pl.pallas_call(
        kernel,
        out_shape=(jax.ShapeDtypeStruct((64, D), bf16), jax.ShapeDtypeStruct((256, 208), bf16)),
        in_specs=[vm] * 8,
        out_specs=(vm, vm),
        scratch_shapes=[
            pltpu.VMEM((2, Z, 128, D + 128), bf16),
            pltpu.VMEM((64, D), bf16),
            pltpu.VMEM((32, 128), bf16),
            pltpu.VMEM((128, 128), f32),
            pltpu.VMEM((2048, 128), bf16),
            pltpu.VMEM((2048, 128), bf16),
            pltpu.VMEM((1024, 128), bf16),
            pltpu.VMEM((1024, 1), f32),
            pltpu.VMEM((1024, 128), f32),
            pltpu.VMEM((16, 64, 128), bf16),
            pltpu.VMEM((16, 64, 128), bf16),
            pltpu.VMEM((NN, 64, 256), bf16),
            pltpu.VMEM((NN, 64, 256), bf16),
            pltpu.VMEM((NN, 128, 256), bf16),
            pltpu.VMEM((NN, 128, 256), bf16),
            pltpu.VMEM((NW, 8, 256), bf16),
            pltpu.VMEM((NW, 8, 256), bf16),
            dma((12,)), dma((X,)), dma((X,)), dma((X,)),
            dma((Z,)), dma((Z,)), dma((Z,)), dma((Z,)),
            dma((16,)), dma((16,)), dma((NN,)), dma((NN,)), dma((NN,)), dma((NN,)),
            dma((NW,)), dma((NW,)),
        ],
        compiler_params=pltpu.CompilerParams(collective_id=0, has_side_effects=True,
                                             vmem_limit_bytes=60 * 1024 * 1024),
    )(queries, keys, values, segment_ids.reshape(1, 128), owners.reshape(1, 128), hidden_in, wout, wm)


def solution(mesh):
    return jax.shard_map(
        shards,
        mesh=mesh,
        in_specs=(
            P(("wide", "narrow"), None),
            P("narrow", "wide", None),
            P("narrow", "wide", None),
            P("narrow", "wide", None),
            P("narrow", "wide"),
            P(None, "narrow", "wide"),
            P("wide"),
            P("wide", None),
        ),
        out_specs=(P(("wide", "narrow"), None), P("wide", "narrow")),
        check_vma=False,
    )
```

```python
import math

import jax
import jax.numpy as jnp
from jax import lax
from jax.experimental import pallas as pl
from jax.experimental.pallas import tpu as pltpu
from jax.sharding import PartitionSpec as P

HD = 104
X, Z, Y = 4, 8, 4
NW, NN = 32, 8
D = 1664
TILE = 2048
BIG = 2.0**100
bf16, f32, i32 = jnp.bfloat16, jnp.float32, jnp.int32
MESH = pl.DeviceIdType.MESH


def iota(shape, dim):
    return lax.broadcasted_iota(i32, shape, dim)


def kernel(q_ref, k_ref, v_ref, seg_ref, own_ref, hin_ref, wo_ref, wm_ref,
           hout_ref, dout_ref,
           kv, qb, oh, tr, kx, vx, qx, m_s, acc_s, ob, orecv, hb, hrecv, fb, frecv, outg, drecv, res, wo, wm,
           s0, r_kv, r_q, r_oh, ss, rs, dss, drs, so, ro, sh, rh, sf, rf, sd, rd,
           swz, rwz, smz, rmz, swx, rwx, smx, rmx, swy, rwy, swp, rwp):
    w = lax.axis_index("wide")
    n = lax.axis_index("narrow")
    x, z = w // Z, w % Z
    y, c = n // 2, n % 2
    up = 1 - 2 * c
    scale = math.log2(math.e) / math.sqrt(HD)

    def is_me(dw, dn):
        return (dw == w) & (dn == n)

    def remote(src, dst, ssem, rsem, dw, dn):
        return pltpu.make_async_remote_copy(src_ref=src, dst_ref=dst, send_sem=ssem, recv_sem=rsem,
                                            device_id=(dw, dn), device_id_type=MESH)

    def send(src, dst, ssem, rsem, dw, dn):
        @pl.when(jnp.logical_not(is_me(dw, dn)))
        def _():
            remote(src, dst, ssem, rsem, dw, dn).start()

        @pl.when(is_me(dw, dn))
        def _():
            pltpu.make_async_copy(src, dst, rsem).start()

    def sent(src, ssem, dw, dn):
        @pl.when(jnp.logical_not(is_me(dw, dn)))
        def _():
            remote(src, src, ssem, ssem, dw, dn).wait_send()

    def arrived(dst, rsem):
        remote(dst, dst, rsem, rsem, w, n).wait_recv()

    barrier = pltpu.get_barrier_semaphore()

    @pl.loop(0, X * NN)
    def _(i):
        dw, dn = (i // NN) * Z + z, i % NN

        @pl.when(jnp.logical_not(is_me(dw, dn)))
        def _():
            pl.semaphore_signal(barrier, inc=1, device_id=(dw, dn), device_id_type=MESH)

    @pl.loop(0, NW)
    def _(i):
        @pl.when(i % Z != z)
        def _():
            pl.semaphore_signal(barrier, inc=1, device_id=(i, n), device_id_type=MESH)

    t = (iota((128, 128), 0) == seg_ref[...] + 32 * (iota((1, 128), 1) & 3)).astype(f32)
    tr[...] = t.T
    oh[...] = (tr[pl.ds(0, 32, stride=4), :] + tr[pl.ds(1, 32, stride=4), :]
               + tr[pl.ds(2, 32, stride=4), :] + tr[pl.ds(3, 32, stride=4), :]).astype(bf16)

    g64, p64 = iota((64, 64), 0), iota((64, 64), 1)
    perm = (p64 == 4 * (g64 & 15) + (g64 >> 4)).astype(bf16)
    hp = jnp.dot(perm, hin_ref[...], preferred_element_type=f32).astype(bf16)
    a208, b208 = iota((208, 256), 0), iota((208, 256), 1)
    spread = ((a208 == 52 * (b208 >> 6) + (b208 & 63)) & ((b208 & 63) < 52)).astype(bf16)
    for i in range(NN):
        res[:, 256 * i:256 * i + 256] = jnp.dot(hp[:, 208 * i:208 * i + 208], spread,
                                                preferred_element_type=f32).astype(bf16)

    eye = (iota((64, 52), 0) == iota((64, 52), 1)).astype(bf16)
    heads = (((b208 < HD) & (a208 == b208)) | ((b208 >= 128) & (b208 < 128 + HD) & (a208 == b208 - 24))).astype(bf16)
    plain = (a208 == b208).astype(bf16)

    def turned(block, lanes):
        t = lax.dot_general(eye, block, (((1,), (1,)), ((), ())), preferred_element_type=f32).astype(bf16)
        return jnp.dot(t, lanes, preferred_element_type=f32).astype(bf16)

    wo[n, w] = turned(wo_ref[...], heads)
    for j in range(4):
        wm[w, j] = turned(wm_ref[j], plain)

    def wo_rows(dx):
        return pl.ds(pl.multiple_of(Z * ((x - dx + X) % X), Z), Z)

    def wo_z(d):
        return remote(wo.at[n, w], wo.at[n, w], swz.at[d], rwz.at[d], x * Z + (z + d) % Z, n)

    def wm_z(d):
        return remote(wm.at[w], wm.at[w], smz.at[d], rmz.at[d], x * Z + (z + d) % Z, n)

    def wo_x(dx):
        ref = wo.at[n, wo_rows(0)]
        return remote(ref, ref, swx.at[dx], rwx.at[dx], ((x + dx) % X) * Z + z, n)

    def wm_x(d, dx):
        ref = wm.at[x * Z + (z - d + Z) % Z]
        return remote(ref, ref, smx.at[4 * d + dx], rmx.at[4 * d + dx], ((x + dx) % X) * Z + z, n)

    def wo_y(dx, dy):
        ref = wo.at[n, wo_rows(dx)]
        return remote(ref, ref, swy.at[4 * dx + dy], rwy.at[4 * dx + dy], w, 2 * ((y + dy) % Y) + c)

    def wo_p(dx, dy):
        ref = wo.at[2 * ((y - dy + Y) % Y) + c, wo_rows(dx)]
        return remote(ref, ref, swp.at[4 * dx + dy], rwp.at[4 * dx + dy], w, n + up)

    def wo_on(dx):
        for dy in range(1, Y):
            wo_y(dx, dy).start()
        wo_p(dx, 0).start()

    owner_row = own_ref[...]
    owner_col = jnp.broadcast_to(owner_row.astype(f32), (128, 128)).T
    same = (owner_col == owner_row.astype(f32)) & (iota((128, 128), 0) < iota((128, 128), 1))
    rank = jnp.sum(same.astype(f32), axis=0, keepdims=True)
    slot_of = owner_row * 8 + rank.astype(i32)
    picker = (iota((256, 128), 0) == slot_of).astype(bf16)

    pl.semaphore_wait(barrier, X * NN - 1 + NW - X)

    rows_x = pl.ds(pl.multiple_of(32 * x, 32), 32)
    rows_q = pl.ds(pl.multiple_of(16 * x, 16), 16)
    main, tail = pl.ds(0, D), pl.ds(D, 128)
    starts = []
    for i in range(2):
        dw = (2 * c + i) * Z + z
        starts.append((k_ref.at[i], kv.at[0, z, rows_x, main], s0.at[i], r_kv.at[x], dw, 2 * y))
        starts.append((v_ref.at[i], kv.at[1, z, rows_x, main], s0.at[2 + i], r_kv.at[x], dw, 2 * y + 1))
    for i in range(2):
        dw = (2 * c + i) * Z + z
        for d in range(2):
            starts.append((q_ref.at[i, pl.ds(16 * d, 16)], qb.at[rows_q], s0.at[4 + 2 * i + d], r_q.at[x], dw,
                           2 * y + d))
    for dx in range(X):
        starts.append((oh, kv.at[c, z, rows_x, tail], s0.at[8 + dx], r_oh.at[x], dx * Z + z, n))
    for args in starts:
        send(*args)

    @pl.loop(1, Z)
    def _(d):
        wo_z(d).start()

    m_s[...] = jnp.full_like(m_s, -3e38)
    acc_s[...] = jnp.zeros_like(acc_s)

    lane = iota((128, 128), 1)
    ones_col = (lane == HD).astype(bf16)

    def piece(ref_slice, j):
        t, r = (HD * j) // 128, (HD * j) % 128
        out = ref_slice(t)
        if r:
            out = pltpu.roll(out, 128 - r, 1)
        if r + HD > 128:
            nxt = pltpu.roll(ref_slice(t + 1), 128 - r, 1)
            out = jnp.where(iota(out.shape, 1) < 128 - r, out, nxt)
        return out

    def attend(slot):
        ohs = kv[0, slot, :, D:D + 128]
        for jj in range(4):
            ohr = pltpu.roll(ohs, (HD - 32 * jj) % 128, 1)
            for j in range(4 * jj, 4 * jj + 4):
                kj = piece(lambda t: kv[0, slot, :, 128 * t:128 * t + 128], j)
                kx[128 * j:128 * j + 128, :] = jnp.where(lane < HD, kj, ohr)
                vj = piece(lambda t: kv[1, slot, :, 128 * t:128 * t + 128], j)
                vx[128 * j:128 * j + 128, :] = jnp.where(lane < HD, vj, ones_col)

        @pl.loop(0, X)
        def _(qt):
            rows = pl.ds(pl.multiple_of(256 * qt, 256), 256)
            s = lax.dot_general(qx[rows, :], kx[...], (((1,), (1,)), ((), ())), preferred_element_type=f32)
            m_old = m_s[rows, :]
            m_new = jnp.maximum(m_old, jnp.max(s, axis=1, keepdims=True))
            p = jnp.exp2((s - m_new) * scale).astype(bf16)
            fix = jnp.exp2((m_old - m_new) * scale)
            acc_s[rows, :] = acc_s[rows, :] * fix + jnp.dot(p, vx[...], preferred_element_type=f32)
            m_s[rows, :] = m_new

    for i in range(X):
        arrived(kv.at[c, z, pl.ds(32 * i, 32), main], r_kv.at[i])
        arrived(kv.at[c, z, pl.ds(32 * i, 32), tail], r_oh.at[i])

    def slot_at(k):
        h = (k + 1) // 2
        sign = jnp.where(k % 2 == 1, -1, 1)
        return (z + sign * up * h + 2 * Z) % Z

    def to_partner(slot):
        return remote(kv.at[c, slot], kv.at[c, slot], dss.at[slot], drs.at[slot], w, n + up)

    def onward(k, t):
        slot = slot_at(k)
        step = jnp.where(t % 2 == 1, up, -up)
        dz = (z + step + Z) % Z
        return remote(kv.at[c, slot], kv.at[c, slot], ss.at[t], rs.at[t], x * Z + dz, n)

    onward(0, 1).start()
    onward(0, 2).start()
    to_partner(z).start()

    @pl.loop(1, Z)
    def _(d):
        wm_z(d).start()

    for i in range(X):
        arrived(qb.at[pl.ds(16 * i, 16)], r_q.at[i])
    lane16 = iota((16, 128), 1)
    for i in range(X):
        ohq = kv[c, z, pl.ds(pl.multiple_of(32 * i + 16 * c, 16), 16), D:D + 128]
        for jj in range(4):
            ohr = (pltpu.roll(ohq, (HD - 32 * jj) % 128, 1) - bf16(1)) * bf16(BIG)
            ohr = jnp.where(lane16 < HD + 16, ohr, bf16(0))
            for j in range(4 * jj, 4 * jj + 4):
                qj = piece(lambda t: qb[16 * i:16 * i + 16, 128 * t:128 * t + 128], j)
                qx[256 * i + 16 * j:256 * i + 16 * j + 16, :] = jnp.where(lane16 < HD, qj, ohr)

    @pl.loop(1, Z)
    def _(d):
        arrived(wo.at[n, x * Z + (z - d + Z) % Z], rwz.at[d])
    for dx in range(1, X):
        wo_x(dx).start()
        wm_x(0, dx).start()
    wo_on(0)

    @pl.loop(0, Z)
    def _(k):
        def take(kk):
            slot = slot_at(kk)
            arrived(kv.at[c, slot], rs.at[kk])

            @pl.when(kk + 2 < Z)
            def _():
                onward(kk, kk + 2).start()
            to_partner(slot).start()

        @pl.when(k % 2 == 1)
        def _():
            take(k)

            @pl.when(k + 1 < Z)
            def _():
                take(k + 1)
        slot = slot_at(k)
        arrived(kv.at[1 - c, slot], drs.at[slot])
        attend(slot)

        @pl.when(k >= 1)
        def _():
            h = (k + 1) // 2
            d = jnp.where(k % 2 == 1, h, Z - h)
            arrived(wm.at[x * Z + (z - d + Z) % Z], rmz.at[d])
            for dx in range(1, X):
                wm_x(d, dx).start()

        @pl.when((k >= 1) & (k < X))
        def _():
            arrived(wo.at[n, wo_rows(k)], rwx.at[k])
            wo_on(k)

        @pl.when(k >= X)
        def _():
            for dy in range(1, Y):
                arrived(wo.at[2 * ((y - dy + Y) % Y) + c, wo_rows(k - X)], rwy.at[4 * (k - X) + dy])
                wo_p(k - X, dy).start()

    i0, i1 = iota((256, 256), 0), iota((256, 256), 1)
    grp, pos = i0 & 15, (i0 >> 4) & 3
    r_src = 4 * (i0 >> 6) + (grp >> 2)
    j_src = 4 * (grp & 3) + pos
    perm256 = (i1 == j_src * 16 + r_src).astype(bf16)
    lane256 = iota((256, 128), 1)
    for i in range(X):
        a = acc_s[256 * i:256 * i + 256, :]
        a = jnp.where(lane256 < HD, a / a[:, HD:HD + 1], 0.0).astype(bf16)
        ob[4 * i:4 * i + 4] = jnp.dot(perm256, a, preferred_element_type=f32).astype(bf16).reshape(4, 64, 128)
    head = 4 * y + x
    for i in range(X):
        for l in range(4):
            send(ob.at[4 * i + l], orecv.at[head], so.at[4 * i + l], ro.at[head], i * Z + z, 4 * c + l)

    @pl.loop(0, X)
    def _(dx):
        for dy in range(Y):
            arrived(wo.at[2 * ((y - dy + Y) % Y) + 1 - c, wo_rows(dx)], rwp.at[4 * dx + dy])
    hid = jnp.zeros((64, TILE), f32)
    for i in range(NN):
        arrived(orecv.at[2 * i], ro.at[2 * i])
        arrived(orecv.at[2 * i + 1], ro.at[2 * i + 1])
        a = jnp.concatenate([orecv[2 * i], orecv[2 * i + 1]], axis=1)
        hid = hid + lax.dot_general(a, wo[i].reshape(TILE, 256), (((1,), (1,)), ((), ())),
                                    preferred_element_type=f32)
    a256, b256 = iota((256, 256), 0), iota((256, 256), 1)
    narrowed = ((b256 == 52 * (a256 >> 6) + (a256 & 63)) & ((a256 & 63) < 52)).astype(bf16)
    for i in range(NN):
        h = (res[:, 256 * i:256 * i + 256].astype(f32) + hid[:, 256 * i:256 * i + 256]).astype(bf16)
        hb[i] = jnp.dot(h, narrowed, preferred_element_type=f32).astype(bf16)
    for i in range(NN):
        send(hb.at[i], hrecv.at[n], sh.at[i], rh.at[n], w, i)
    whole = jnp.concatenate([hb[i][:, 0:208] for i in range(NN)], axis=1)
    back = (g64 == 4 * (p64 & 15) + (p64 >> 4)).astype(bf16)
    hout_ref[...] = jnp.dot(back, whole, preferred_element_type=f32).astype(bf16)

    for i in range(NN):
        arrived(hrecv.at[i], rh.at[i])
    @pl.loop(0, Z)
    def _(d):
        for dx in range(1, X):
            arrived(wm.at[Z * ((x - dx + X) % X) + (z - d + Z) % Z], rmx.at[4 * d + dx])
    part = jnp.zeros((128, TILE), f32)
    for j in range(4):
        part = part + lax.dot_general(hrecv[:, 16 * j:16 * j + 16, :].reshape(128, 256),
                                      wm[:, j].reshape(TILE, 256), (((1,), (1,)), ((), ())),
                                      preferred_element_type=f32)
    for i in range(NN):
        fb[i] = part[:, 256 * i:256 * i + 256].astype(bf16)
    for i in range(NN):
        send(fb.at[i], frecv.at[n], sf.at[i], rf.at[n], w, i)
    feat = jnp.zeros((128, 256), f32)
    for i in range(NN):
        arrived(frecv.at[i], rf.at[i])
        feat = feat + frecv[i].astype(f32)

    feat = jnp.dot(feat.astype(bf16), narrowed, preferred_element_type=f32)
    outg[...] = jnp.dot(picker, feat.astype(bf16), preferred_element_type=f32).reshape(NW, 8, 256).astype(bf16)

    @pl.loop(0, NW)
    def _(i):
        send(outg.at[i], drecv.at[w], sd.at[i], rd.at[w], i, n)

    @pl.loop(0, NW)
    def _(i):
        arrived(drecv.at[i], rd.at[i])
    dout_ref[...] = drecv[...].astype(f32).reshape(256, 256).astype(bf16)[:, 0:208]

    for src, dst, ssem, rsem, dw, dn in starts:
        sent(src, ssem, dw, dn)

    @pl.loop(1, Z)
    def _(t):
        onward(jnp.maximum(t - 2, 0), t).wait_send()
        wo_z(t).wait_send()
        wm_z(t).wait_send()
    for dx in range(1, X):
        wo_x(dx).wait_send()

    @pl.loop(0, Z)
    def _(d):
        for dx in range(1, X):
            wm_x(d, dx).wait_send()

    @pl.loop(0, X)
    def _(dx):
        wo_p(dx, 0).wait_send()
        for dy in range(1, Y):
            wo_y(dx, dy).wait_send()
            wo_p(dx, dy).wait_send()

    @pl.loop(0, Z)
    def _(t):
        to_partner(t).wait_send()
    for i in range(X):
        for l in range(4):
            sent(ob.at[4 * i + l], so.at[4 * i + l], i * Z + z, 4 * c + l)
    for i in range(NN):
        sent(hb.at[i], sh.at[i], w, i)
        sent(fb.at[i], sf.at[i], w, i)

    @pl.loop(0, NW)
    def _(i):
        sent(outg.at[i], sd.at[i], i, n)


def shards(hidden_in, queries, keys, values, out_weight, merge_weight, segment_ids, owners):
    vm = pl.BlockSpec(memory_space=pltpu.VMEM)
    dma = pltpu.SemaphoreType.DMA
    return pl.pallas_call(
        kernel,
        out_shape=(jax.ShapeDtypeStruct((64, D), bf16), jax.ShapeDtypeStruct((256, 208), bf16)),
        in_specs=[vm] * 8,
        out_specs=(vm, vm),
        scratch_shapes=[
            pltpu.VMEM((2, Z, 128, D + 128), bf16),
            pltpu.VMEM((64, D), bf16),
            pltpu.VMEM((32, 128), bf16),
            pltpu.VMEM((128, 128), f32),
            pltpu.VMEM((2048, 128), bf16),
            pltpu.VMEM((2048, 128), bf16),
            pltpu.VMEM((1024, 128), bf16),
            pltpu.VMEM((1024, 1), f32),
            pltpu.VMEM((1024, 128), f32),
            pltpu.VMEM((16, 64, 128), bf16),
            pltpu.VMEM((16, 64, 128), bf16),
            pltpu.VMEM((NN, 64, 256), bf16),
            pltpu.VMEM((NN, 64, 256), bf16),
            pltpu.VMEM((NN, 128, 256), bf16),
            pltpu.VMEM((NN, 128, 256), bf16),
            pltpu.VMEM((NW, 8, 256), bf16),
            pltpu.VMEM((NW, 8, 256), bf16),
            pltpu.VMEM((64, TILE), bf16),
            pltpu.VMEM((NN, NW, 64, 256), bf16),
            pltpu.VMEM((NW, 4, 64, 256), bf16),
            dma((12,)), dma((X,)), dma((X,)), dma((X,)),
            dma((Z,)), dma((Z,)), dma((Z,)), dma((Z,)),
            dma((16,)), dma((16,)), dma((NN,)), dma((NN,)), dma((NN,)), dma((NN,)),
            dma((NW,)), dma((NW,)),
            dma((Z,)), dma((Z,)), dma((Z,)), dma((Z,)), dma((X,)), dma((X,)), dma((4 * Z,)), dma((4 * Z,)),
            dma((16,)), dma((16,)), dma((16,)), dma((16,)),
        ],
        compiler_params=pltpu.CompilerParams(collective_id=0, has_side_effects=True,
                                             vmem_limit_bytes=60 * 1024 * 1024),
    )(queries, keys, values, segment_ids.reshape(1, 128), owners.reshape(1, 128), hidden_in, out_weight, merge_weight)


def solution(mesh):
    return jax.shard_map(
        shards,
        mesh=mesh,
        in_specs=(
            P(("wide", "narrow"), None),
            P("narrow", "wide", None),
            P("narrow", "wide", None),
            P("narrow", "wide", None),
            P("narrow", "wide"),
            P(None, "narrow", "wide"),
            P("wide"),
            P("wide", None),
        ),
        out_specs=(P(("wide", "narrow"), None), P("wide", "narrow")),
        check_vma=False,
    )
```

```python
import math

import jax
import jax.numpy as jnp
from jax import lax
from jax.experimental import pallas as pl
from jax.experimental.pallas import tpu as pltpu
from jax.sharding import PartitionSpec as P

HD = 104
X, Z, Y = 4, 8, 4
NW, NN = 32, 8
D = 1664
TILE = 2048
BIG = 2.0**100
bf16, f32, i32 = jnp.bfloat16, jnp.float32, jnp.int32
MESH = pl.DeviceIdType.MESH


def iota(shape, dim):
    return lax.broadcasted_iota(i32, shape, dim)


def kernel(q_ref, k_ref, v_ref, seg_ref, own_ref, hin_ref, wo_ref, wm_ref,
           hout_ref, dout_ref,
           kv, qb, oh, tr, kx, vx, qx, m_s, acc_s, ob, orecv, hb, hrecv, fb, frecv, outg, drecv, res, wo, wm,
           s0, r_kv, r_q, r_oh, ss, rs, dss, drs, so, ro, sh, rh, sf, rf, sd, rd,
           swz, rwz, smz, rmz, swx, rwx, smx, rmx, swy, rwy, swp, rwp):
    w = lax.axis_index("wide")
    n = lax.axis_index("narrow")
    x, z = w // Z, w % Z
    y, c = n // 2, n % 2
    up = 1 - 2 * c
    scale = math.log2(math.e) / math.sqrt(HD)

    def is_me(dw, dn):
        return (dw == w) & (dn == n)

    def remote(src, dst, ssem, rsem, dw, dn):
        return pltpu.make_async_remote_copy(src_ref=src, dst_ref=dst, send_sem=ssem, recv_sem=rsem,
                                            device_id=(dw, dn), device_id_type=MESH)

    def send(src, dst, ssem, rsem, dw, dn):
        @pl.when(jnp.logical_not(is_me(dw, dn)))
        def _():
            remote(src, dst, ssem, rsem, dw, dn).start()

        @pl.when(is_me(dw, dn))
        def _():
            pltpu.make_async_copy(src, dst, rsem).start()

    def sent(src, ssem, dw, dn):
        @pl.when(jnp.logical_not(is_me(dw, dn)))
        def _():
            remote(src, src, ssem, ssem, dw, dn).wait_send()

    def arrived(dst, rsem):
        remote(dst, dst, rsem, rsem, w, n).wait_recv()

    barrier = pltpu.get_barrier_semaphore()

    @pl.loop(0, X * NN)
    def _(i):
        dw, dn = (i // NN) * Z + z, i % NN

        @pl.when(jnp.logical_not(is_me(dw, dn)))
        def _():
            pl.semaphore_signal(barrier, inc=1, device_id=(dw, dn), device_id_type=MESH)

    @pl.loop(0, NW)
    def _(i):
        @pl.when(i % Z != z)
        def _():
            pl.semaphore_signal(barrier, inc=1, device_id=(i, n), device_id_type=MESH)

    t = (iota((128, 128), 0) == seg_ref[...] + 32 * (iota((1, 128), 1) & 3)).astype(f32)
    tr[...] = t.T
    oh[...] = (tr[pl.ds(0, 32, stride=4), :] + tr[pl.ds(1, 32, stride=4), :]
               + tr[pl.ds(2, 32, stride=4), :] + tr[pl.ds(3, 32, stride=4), :]).astype(bf16)

    g64, p64 = iota((64, 64), 0), iota((64, 64), 1)
    perm = (p64 == 4 * (g64 & 15) + (g64 >> 4)).astype(bf16)
    hp = jnp.dot(perm, hin_ref[...], preferred_element_type=f32).astype(bf16)
    a208, b208 = iota((208, 256), 0), iota((208, 256), 1)
    spread = ((a208 == 52 * (b208 >> 6) + (b208 & 63)) & ((b208 & 63) < 52)).astype(bf16)
    for i in range(NN):
        res[:, 256 * i:256 * i + 256] = jnp.dot(hp[:, 208 * i:208 * i + 208], spread,
                                                preferred_element_type=f32).astype(bf16)

    eye = (iota((64, 52), 0) == iota((64, 52), 1)).astype(bf16)
    heads = (((b208 < HD) & (a208 == b208)) | ((b208 >= 128) & (b208 < 128 + HD) & (a208 == b208 - 24))).astype(bf16)
    plain = (a208 == b208).astype(bf16)

    def turned(block, lanes):
        t = lax.dot_general(eye, block, (((1,), (1,)), ((), ())), preferred_element_type=f32).astype(bf16)
        return jnp.dot(t, lanes, preferred_element_type=f32).astype(bf16)

    wo[n, w] = turned(wo_ref[...], heads)
    for j in range(4):
        wm[w, j] = turned(wm_ref[j], plain)

    def wo_rows(dx):
        return pl.ds(pl.multiple_of(Z * ((x - dx + X) % X), Z), Z)

    def wo_z(d):
        return remote(wo.at[n, w], wo.at[n, w], swz.at[d], rwz.at[d], x * Z + (z + d) % Z, n)

    def slot_at(k):
        h = (k + 1) // 2
        sign = jnp.where(k % 2 == 1, -1, 1)
        return (z + sign * up * h + 2 * Z) % Z

    def wm_z(k, t):
        ref = wm.at[x * Z + slot_at(k)]
        dz = (z + jnp.where(t % 2 == 1, up, -up) + Z) % Z
        return remote(ref, ref, smz.at[t], rmz.at[t], x * Z + dz, n)

    def half_rows(dx, i):
        return pl.ds(pl.multiple_of(Z * ((x - dx + X) % X) + 4 * i, 4), 4)

    def wo_x(dx):
        ref = wo.at[n, wo_rows(0)]
        return remote(ref, ref, swx.at[dx], rwx.at[dx], ((x + dx) % X) * Z + z, n)

    def wo_xr(i):
        ref = wo.at[n, half_rows(1 + 2 * i, i)]
        return remote(ref, ref, swx.at[2 * i], rwx.at[2 * i], ((x + 1 + 2 * i) % X) * Z + z, n)

    def wm_at(k, dx):
        return wm.at[Z * ((x - dx + X) % X) + slot_at(k)]

    def wm_half(k, dx, i):
        return wm.at[Z * ((x - dx + X) % X) + slot_at(k), pl.ds(2 * i, 2)]

    def wm_x(k, dx):
        ref = wm_at(k, 0)
        return remote(ref, ref, smx.at[4 * k + dx], rmx.at[4 * k + dx], ((x + dx) % X) * Z + z, n)

    def wm_xr(k, i):
        ref = wm_half(k, 1 + 2 * i, i)
        return remote(ref, ref, smx.at[4 * k + 2 * i], rmx.at[4 * k + 2 * i], ((x + 1 + 2 * i) % X) * Z + z, n)

    def wm_relay(k):
        for i in range(2):
            arrived(wm_at(k, 1 + 2 * i), rmx.at[4 * k + 1 + 2 * i])
            wm_xr(k, i).start()

    def narrow_at(dy):
        return 2 * ((y - dy + Y) % Y) + c

    def wo_y(dx, dy):
        ref = wo.at[n, wo_rows(dx)]
        return remote(ref, ref, swy.at[4 * dx + dy], rwy.at[4 * dx + dy], w, 2 * ((y + dy) % Y) + c)

    def wo_yr(dx, i):
        ref = wo.at[narrow_at(1 + 2 * i), half_rows(dx, i)]
        return remote(ref, ref, swy.at[4 * dx + 2 * i], rwy.at[4 * dx + 2 * i], w, 2 * ((y + 1 + 2 * i) % Y) + c)

    def wo_p(dx, dy):
        ref = wo.at[narrow_at(dy), wo_rows(dx)]
        return remote(ref, ref, swp.at[4 * dx + dy], rwp.at[4 * dx + dy], w, n + up)

    def wo_on(dx):
        wo_y(dx, 1).start()
        wo_y(dx, 3).start()
        wo_p(dx, 0).start()

    def wo_relay(dx):
        for i in range(2):
            arrived(wo.at[narrow_at(1 + 2 * i), wo_rows(dx)], rwy.at[4 * dx + 1 + 2 * i])
            wo_yr(dx, i).start()
            wo_p(dx, 1 + 2 * i).start()

    def wo_last(dx):
        for i in range(2):
            arrived(wo.at[narrow_at(2), half_rows(dx, i)], rwy.at[4 * dx + 2 * i])
        wo_p(dx, 2).start()

    owner_row = own_ref[...]
    owner_col = jnp.broadcast_to(owner_row.astype(f32), (128, 128)).T
    same = (owner_col == owner_row.astype(f32)) & (iota((128, 128), 0) < iota((128, 128), 1))
    rank = jnp.sum(same.astype(f32), axis=0, keepdims=True)
    slot_of = owner_row * 8 + rank.astype(i32)
    picker = (iota((256, 128), 0) == slot_of).astype(bf16)

    pl.semaphore_wait(barrier, X * NN - 1 + NW - X)

    rows_x = pl.ds(pl.multiple_of(32 * x, 32), 32)
    rows_q = pl.ds(pl.multiple_of(16 * x, 16), 16)
    main, tail = pl.ds(0, D), pl.ds(D, 128)
    starts = []
    for i in range(2):
        dw = (2 * c + i) * Z + z
        starts.append((k_ref.at[i], kv.at[0, z, rows_x, main], s0.at[i], r_kv.at[x], dw, 2 * y))
        starts.append((v_ref.at[i], kv.at[1, z, rows_x, main], s0.at[2 + i], r_kv.at[x], dw, 2 * y + 1))
    for i in range(2):
        dw = (2 * c + i) * Z + z
        for d in range(2):
            starts.append((q_ref.at[i, pl.ds(16 * d, 16)], qb.at[rows_q], s0.at[4 + 2 * i + d], r_q.at[x], dw,
                           2 * y + d))
    for dx in range(X):
        starts.append((oh, kv.at[c, z, rows_x, tail], s0.at[8 + dx], r_oh.at[x], dx * Z + z, n))
    for args in starts:
        send(*args)

    @pl.loop(1, Z)
    def _(d):
        wo_z(d).start()

    m_s[...] = jnp.full_like(m_s, -3e38)
    acc_s[...] = jnp.zeros_like(acc_s)

    lane = iota((128, 128), 1)
    ones_col = (lane == HD).astype(bf16)

    def piece(ref_slice, j):
        t, r = (HD * j) // 128, (HD * j) % 128
        out = ref_slice(t)
        if r:
            out = pltpu.roll(out, 128 - r, 1)
        if r + HD > 128:
            nxt = pltpu.roll(ref_slice(t + 1), 128 - r, 1)
            out = jnp.where(iota(out.shape, 1) < 128 - r, out, nxt)
        return out

    def attend(slot):
        ohs = kv[0, slot, :, D:D + 128]
        for jj in range(4):
            ohr = pltpu.roll(ohs, (HD - 32 * jj) % 128, 1)
            for j in range(4 * jj, 4 * jj + 4):
                kj = piece(lambda t: kv[0, slot, :, 128 * t:128 * t + 128], j)
                kx[128 * j:128 * j + 128, :] = jnp.where(lane < HD, kj, ohr)
                vj = piece(lambda t: kv[1, slot, :, 128 * t:128 * t + 128], j)
                vx[128 * j:128 * j + 128, :] = jnp.where(lane < HD, vj, ones_col)

        @pl.loop(0, X)
        def _(qt):
            rows = pl.ds(pl.multiple_of(256 * qt, 256), 256)
            s = lax.dot_general(qx[rows, :], kx[...], (((1,), (1,)), ((), ())), preferred_element_type=f32)
            m_old = m_s[rows, :]
            m_new = jnp.maximum(m_old, jnp.max(s, axis=1, keepdims=True))
            p = jnp.exp2((s - m_new) * scale).astype(bf16)
            fix = jnp.exp2((m_old - m_new) * scale)
            acc_s[rows, :] = acc_s[rows, :] * fix + jnp.dot(p, vx[...], preferred_element_type=f32)
            m_s[rows, :] = m_new

    for i in range(X):
        arrived(kv.at[c, z, pl.ds(32 * i, 32), main], r_kv.at[i])
        arrived(kv.at[c, z, pl.ds(32 * i, 32), tail], r_oh.at[i])

    def to_partner(slot):
        return remote(kv.at[c, slot], kv.at[c, slot], dss.at[slot], drs.at[slot], w, n + up)

    def onward(k, t):
        slot = slot_at(k)
        step = jnp.where(t % 2 == 1, up, -up)
        dz = (z + step + Z) % Z
        return remote(kv.at[c, slot], kv.at[c, slot], ss.at[t], rs.at[t], x * Z + dz, n)

    onward(0, 1).start()
    onward(0, 2).start()
    to_partner(z).start()

    wm_z(0, 1).start()
    wm_z(0, 2).start()

    for i in range(X):
        arrived(qb.at[pl.ds(16 * i, 16)], r_q.at[i])
    lane16 = iota((16, 128), 1)
    for i in range(X):
        ohq = kv[c, z, pl.ds(pl.multiple_of(32 * i + 16 * c, 16), 16), D:D + 128]
        for jj in range(4):
            ohr = (pltpu.roll(ohq, (HD - 32 * jj) % 128, 1) - bf16(1)) * bf16(BIG)
            ohr = jnp.where(lane16 < HD + 16, ohr, bf16(0))
            for j in range(4 * jj, 4 * jj + 4):
                qj = piece(lambda t: qb[16 * i:16 * i + 16, 128 * t:128 * t + 128], j)
                qx[256 * i + 16 * j:256 * i + 16 * j + 16, :] = jnp.where(lane16 < HD, qj, ohr)

    @pl.loop(1, Z)
    def _(d):
        arrived(wo.at[n, x * Z + (z - d + Z) % Z], rwz.at[d])
    for dx in (1, 3):
        wo_x(dx).start()
        wm_x(0, dx).start()
    wo_on(0)

    @pl.loop(0, Z)
    def _(k):
        def take(kk):
            slot = slot_at(kk)
            arrived(kv.at[c, slot], rs.at[kk])

            @pl.when(kk + 2 < Z)
            def _():
                onward(kk, kk + 2).start()
            to_partner(slot).start()

        @pl.when(k % 2 == 1)
        def _():
            take(k)

            @pl.when(k + 1 < Z)
            def _():
                take(k + 1)
        slot = slot_at(k)
        arrived(kv.at[1 - c, slot], drs.at[slot])
        attend(slot)

        @pl.when(k >= 1)
        def _():
            arrived(wm_at(k, 0), rmz.at[k])

            @pl.when(k + 2 < Z)
            def _():
                wm_z(k, k + 2).start()
            for dx in (1, 3):
                wm_x(k, dx).start()

        @pl.when(k == 1)
        def _():
            for i in range(2):
                arrived(wo.at[n, wo_rows(1 + 2 * i)], rwx.at[1 + 2 * i])
                wo_xr(i).start()

        @pl.when(k == 3)
        def _():
            for i in range(2):
                arrived(wo.at[n, half_rows(2, i)], rwx.at[2 * i])

        def nth(i):
            return i + jnp.where(i == 2, 1, 0) - jnp.where(i == 3, 1, 0)

        @pl.when((k >= 1) & (k < X))
        def _():
            wo_on(nth(k))

        @pl.when((k >= 1) & (k < X + 1))
        def _():
            wo_relay(nth(k - 1))

        @pl.when((k >= 2) & (k < X + 2))
        def _():
            wo_last(nth(k - 2))

        @pl.when(k >= 1)
        def _():
            wm_relay(k - 1)

    i0, i1 = iota((256, 256), 0), iota((256, 256), 1)
    grp, pos = i0 & 15, (i0 >> 4) & 3
    r_src = 4 * (i0 >> 6) + (grp >> 2)
    j_src = 4 * (grp & 3) + pos
    perm256 = (i1 == j_src * 16 + r_src).astype(bf16)
    lane256 = iota((256, 128), 1)
    for i in range(X):
        a = acc_s[256 * i:256 * i + 256, :]
        a = jnp.where(lane256 < HD, a / a[:, HD:HD + 1], 0.0).astype(bf16)
        ob[4 * i:4 * i + 4] = jnp.dot(perm256, a, preferred_element_type=f32).astype(bf16).reshape(4, 64, 128)
    head = 4 * y + x
    for i in range(X):
        for l in range(4):
            send(ob.at[4 * i + l], orecv.at[head], so.at[4 * i + l], ro.at[head], i * Z + z, 4 * c + l)

    wm_relay(Z - 1)

    @pl.loop(0, X)
    def _(dx):
        for dy in range(Y):
            arrived(wo.at[2 * ((y - dy + Y) % Y) + 1 - c, wo_rows(dx)], rwp.at[4 * dx + dy])
    hid = jnp.zeros((64, TILE), f32)
    for i in range(NN):
        arrived(orecv.at[2 * i], ro.at[2 * i])
        arrived(orecv.at[2 * i + 1], ro.at[2 * i + 1])
        a = jnp.concatenate([orecv[2 * i], orecv[2 * i + 1]], axis=1)
        hid = hid + lax.dot_general(a, wo[i].reshape(TILE, 256), (((1,), (1,)), ((), ())),
                                    preferred_element_type=f32)
    a256, b256 = iota((256, 256), 0), iota((256, 256), 1)
    narrowed = ((b256 == 52 * (a256 >> 6) + (a256 & 63)) & ((a256 & 63) < 52)).astype(bf16)
    for i in range(NN):
        h = (res[:, 256 * i:256 * i + 256].astype(f32) + hid[:, 256 * i:256 * i + 256]).astype(bf16)
        hb[i] = jnp.dot(h, narrowed, preferred_element_type=f32).astype(bf16)
    for i in range(NN):
        send(hb.at[i], hrecv.at[n], sh.at[i], rh.at[n], w, i)
    whole = jnp.concatenate([hb[i][:, 0:208] for i in range(NN)], axis=1)
    back = (g64 == 4 * (p64 & 15) + (p64 >> 4)).astype(bf16)
    hout_ref[...] = jnp.dot(back, whole, preferred_element_type=f32).astype(bf16)

    for i in range(NN):
        arrived(hrecv.at[i], rh.at[i])
    @pl.loop(0, Z)
    def _(k):
        for i in range(2):
            arrived(wm_half(k, 2, i), rmx.at[4 * k + 2 * i])
    part = jnp.zeros((128, TILE), f32)
    for j in range(4):
        part = part + lax.dot_general(hrecv[:, 16 * j:16 * j + 16, :].reshape(128, 256),
                                      wm[:, j].reshape(TILE, 256), (((1,), (1,)), ((), ())),
                                      preferred_element_type=f32)
    for i in range(NN):
        fb[i] = part[:, 256 * i:256 * i + 256].astype(bf16)
    for i in range(NN):
        send(fb.at[i], frecv.at[n], sf.at[i], rf.at[n], w, i)
    feat = jnp.zeros((128, 256), f32)
    for i in range(NN):
        arrived(frecv.at[i], rf.at[i])
        feat = feat + frecv[i].astype(f32)

    feat = jnp.dot(feat.astype(bf16), narrowed, preferred_element_type=f32)
    outg[...] = jnp.dot(picker, feat.astype(bf16), preferred_element_type=f32).reshape(NW, 8, 256).astype(bf16)

    @pl.loop(0, NW)
    def _(i):
        send(outg.at[i], drecv.at[w], sd.at[i], rd.at[w], i, n)

    @pl.loop(0, NW)
    def _(i):
        arrived(drecv.at[i], rd.at[i])
    dout_ref[...] = drecv[...].astype(f32).reshape(256, 256).astype(bf16)[:, 0:208]

    for src, dst, ssem, rsem, dw, dn in starts:
        sent(src, ssem, dw, dn)

    @pl.loop(1, Z)
    def _(t):
        onward(jnp.maximum(t - 2, 0), t).wait_send()
        wo_z(t).wait_send()
        wm_z(jnp.maximum(t - 2, 0), t).wait_send()
    for i in range(2):
        wo_x(1 + 2 * i).wait_send()
        wo_xr(i).wait_send()

    @pl.loop(0, Z)
    def _(k):
        for i in range(2):
            wm_x(k, 1 + 2 * i).wait_send()
            wm_xr(k, i).wait_send()

    @pl.loop(0, X)
    def _(dx):
        for i in range(2):
            wo_y(dx, 1 + 2 * i).wait_send()
            wo_yr(dx, i).wait_send()
        for dy in range(Y):
            wo_p(dx, dy).wait_send()

    @pl.loop(0, Z)
    def _(t):
        to_partner(t).wait_send()
    for i in range(X):
        for l in range(4):
            sent(ob.at[4 * i + l], so.at[4 * i + l], i * Z + z, 4 * c + l)
    for i in range(NN):
        sent(hb.at[i], sh.at[i], w, i)
        sent(fb.at[i], sf.at[i], w, i)

    @pl.loop(0, NW)
    def _(i):
        sent(outg.at[i], sd.at[i], i, n)


def shards(hidden_in, queries, keys, values, out_weight, merge_weight, segment_ids, owners):
    vm = pl.BlockSpec(memory_space=pltpu.VMEM)
    dma = pltpu.SemaphoreType.DMA
    return pl.pallas_call(
        kernel,
        out_shape=(jax.ShapeDtypeStruct((64, D), bf16), jax.ShapeDtypeStruct((256, 208), bf16)),
        in_specs=[vm] * 8,
        out_specs=(vm, vm),
        scratch_shapes=[
            pltpu.VMEM((2, Z, 128, D + 128), bf16),
            pltpu.VMEM((64, D), bf16),
            pltpu.VMEM((32, 128), bf16),
            pltpu.VMEM((128, 128), f32),
            pltpu.VMEM((2048, 128), bf16),
            pltpu.VMEM((2048, 128), bf16),
            pltpu.VMEM((1024, 128), bf16),
            pltpu.VMEM((1024, 1), f32),
            pltpu.VMEM((1024, 128), f32),
            pltpu.VMEM((16, 64, 128), bf16),
            pltpu.VMEM((16, 64, 128), bf16),
            pltpu.VMEM((NN, 64, 256), bf16),
            pltpu.VMEM((NN, 64, 256), bf16),
            pltpu.VMEM((NN, 128, 256), bf16),
            pltpu.VMEM((NN, 128, 256), bf16),
            pltpu.VMEM((NW, 8, 256), bf16),
            pltpu.VMEM((NW, 8, 256), bf16),
            pltpu.VMEM((64, TILE), bf16),
            pltpu.VMEM((NN, NW, 64, 256), bf16),
            pltpu.VMEM((NW, 4, 64, 256), bf16),
            dma((12,)), dma((X,)), dma((X,)), dma((X,)),
            dma((Z,)), dma((Z,)), dma((Z,)), dma((Z,)),
            dma((16,)), dma((16,)), dma((NN,)), dma((NN,)), dma((NN,)), dma((NN,)),
            dma((NW,)), dma((NW,)),
            dma((Z,)), dma((Z,)), dma((Z,)), dma((Z,)), dma((X,)), dma((X,)), dma((4 * Z,)), dma((4 * Z,)),
            dma((16,)), dma((16,)), dma((16,)), dma((16,)),
        ],
        compiler_params=pltpu.CompilerParams(collective_id=0, has_side_effects=True,
                                             vmem_limit_bytes=60 * 1024 * 1024),
    )(queries, keys, values, segment_ids.reshape(1, 128), owners.reshape(1, 128), hidden_in, out_weight, merge_weight)


def solution(mesh):
    return jax.shard_map(
        shards,
        mesh=mesh,
        in_specs=(
            P(("wide", "narrow"), None),
            P("narrow", "wide", None),
            P("narrow", "wide", None),
            P("narrow", "wide", None),
            P("narrow", "wide"),
            P(None, "narrow", "wide"),
            P("wide"),
            P("wide", None),
        ),
        out_specs=(P(("wide", "narrow"), None), P("wide", "narrow")),
        check_vma=False,
    )
```

```python
import math

import jax
import jax.numpy as jnp
from jax import lax
from jax.experimental import pallas as pl
from jax.experimental.pallas import tpu as pltpu
from jax.sharding import PartitionSpec as P

HD = 104
X, Z, Y = 4, 8, 4
NW, NN = 32, 8
D = 1664
TILE = 2048
BIG = 2.0**100
bf16, f32, i32 = jnp.bfloat16, jnp.float32, jnp.int32
MESH = pl.DeviceIdType.MESH


def iota(shape, dim):
    return lax.broadcasted_iota(i32, shape, dim)


def kernel(q_ref, k_ref, v_ref, seg_ref, own_ref, hin_ref, wo_ref, wm_ref,
           hout_ref, dout_ref,
           kv, qb, oh, tr, kx, vx, qx, m_s, acc_s, ob, orecv, hb, hrecv, fb, frecv, outg, drecv, res, wo, wm,
           s0, r_kv, r_q, r_oh, ss, rs, dss, drs, so, ro, sh, rh, sf, rf, sd, rd,
           swz, rwz, smz, rmz, swx, rwx, smx, rmx, swy, rwy, swp, rwp):
    w = lax.axis_index("wide")
    n = lax.axis_index("narrow")
    x, z = w // Z, w % Z
    y, c = n // 2, n % 2
    up = 1 - 2 * c
    scale = math.log2(math.e) / math.sqrt(HD)

    def is_me(dw, dn):
        return (dw == w) & (dn == n)

    def remote(src, dst, ssem, rsem, dw, dn):
        return pltpu.make_async_remote_copy(src_ref=src, dst_ref=dst, send_sem=ssem, recv_sem=rsem,
                                            device_id=(dw, dn), device_id_type=MESH)

    def send(src, dst, ssem, rsem, dw, dn):
        @pl.when(jnp.logical_not(is_me(dw, dn)))
        def _():
            remote(src, dst, ssem, rsem, dw, dn).start()

        @pl.when(is_me(dw, dn))
        def _():
            pltpu.make_async_copy(src, dst, rsem).start()

    def sent(src, ssem, dw, dn):
        @pl.when(jnp.logical_not(is_me(dw, dn)))
        def _():
            remote(src, src, ssem, ssem, dw, dn).wait_send()

    def arrived(dst, rsem):
        remote(dst, dst, rsem, rsem, w, n).wait_recv()

    barrier = pltpu.get_barrier_semaphore()

    @pl.loop(0, X * NN)
    def _(i):
        dw, dn = (i // NN) * Z + z, i % NN

        @pl.when(jnp.logical_not(is_me(dw, dn)))
        def _():
            pl.semaphore_signal(barrier, inc=1, device_id=(dw, dn), device_id_type=MESH)

    @pl.loop(0, NW)
    def _(i):
        @pl.when(i % Z != z)
        def _():
            pl.semaphore_signal(barrier, inc=1, device_id=(i, n), device_id_type=MESH)

    t = (iota((128, 128), 0) == seg_ref[...] + 32 * (iota((1, 128), 1) & 3)).astype(f32)
    tr[...] = t.T
    oh[...] = (tr[pl.ds(0, 32, stride=4), :] + tr[pl.ds(1, 32, stride=4), :]
               + tr[pl.ds(2, 32, stride=4), :] + tr[pl.ds(3, 32, stride=4), :]).astype(bf16)

    g64, p64 = iota((64, 64), 0), iota((64, 64), 1)
    perm = (p64 == 4 * (g64 & 15) + (g64 >> 4)).astype(bf16)
    hp = jnp.dot(perm, hin_ref[...], preferred_element_type=f32).astype(bf16)
    a208, b208 = iota((208, 256), 0), iota((208, 256), 1)
    spread = ((a208 == 52 * (b208 >> 6) + (b208 & 63)) & ((b208 & 63) < 52)).astype(bf16)
    for i in range(NN):
        res[:, 256 * i:256 * i + 256] = jnp.dot(hp[:, 208 * i:208 * i + 208], spread,
                                                preferred_element_type=f32).astype(bf16)

    eye = (iota((64, 52), 0) == iota((64, 52), 1)).astype(bf16)
    heads = (((b208 < HD) & (a208 == b208)) | ((b208 >= 128) & (b208 < 128 + HD) & (a208 == b208 - 24))).astype(bf16)
    plain = (a208 == b208).astype(bf16)

    def turned(block, lanes):
        t = lax.dot_general(eye, block, (((1,), (1,)), ((), ())), preferred_element_type=f32).astype(bf16)
        return jnp.dot(t, lanes, preferred_element_type=f32).astype(bf16)

    wo[n, w] = turned(wo_ref[...], heads)
    for j in range(4):
        wm[w, j] = turned(wm_ref[j], plain)

    def wo_rows(dx):
        return pl.ds(pl.multiple_of(Z * ((x - dx + X) % X), Z), Z)

    def wo_z(d):
        return remote(wo.at[n, w], wo.at[n, w], swz.at[d], rwz.at[d], x * Z + (z + d) % Z, n)

    def slot_at(k):
        h = (k + 1) // 2
        sign = jnp.where(k % 2 == 1, -1, 1)
        return (z + sign * up * h + 2 * Z) % Z

    def wm_z(k, t):
        ref = wm.at[x * Z + slot_at(k)]
        dz = (z + jnp.where(t % 2 == 1, up, -up) + Z) % Z
        return remote(ref, ref, smz.at[t], rmz.at[t], x * Z + dz, n)

    def half_rows(dx, i):
        return pl.ds(pl.multiple_of(Z * ((x - dx + X) % X) + 4 * i, 4), 4)

    def wo_x(dx):
        ref = wo.at[n, wo_rows(0)]
        return remote(ref, ref, swx.at[dx], rwx.at[dx], ((x + dx) % X) * Z + z, n)

    def wo_xr(i):
        ref = wo.at[n, half_rows(1 + 2 * i, i)]
        return remote(ref, ref, swx.at[2 * i], rwx.at[2 * i], ((x + 1 + 2 * i) % X) * Z + z, n)

    def wm_at(k, dx):
        return wm.at[Z * ((x - dx + X) % X) + slot_at(k)]

    def wm_half(k, dx, i):
        return wm.at[Z * ((x - dx + X) % X) + slot_at(k), pl.ds(2 * i, 2)]

    def wm_x(k, dx):
        ref = wm_at(k, 0)
        return remote(ref, ref, smx.at[4 * k + dx], rmx.at[4 * k + dx], ((x + dx) % X) * Z + z, n)

    def wm_xr(k, i):
        ref = wm_half(k, 1 + 2 * i, i)
        return remote(ref, ref, smx.at[4 * k + 2 * i], rmx.at[4 * k + 2 * i], ((x + 1 + 2 * i) % X) * Z + z, n)

    def wm_relay(k):
        for i in range(2):
            arrived(wm_at(k, 1 + 2 * i), rmx.at[4 * k + 1 + 2 * i])
            wm_xr(k, i).start()

    def narrow_at(dy):
        return 2 * ((y - dy + Y) % Y) + c

    def wo_y(dx, dy):
        ref = wo.at[n, wo_rows(dx)]
        return remote(ref, ref, swy.at[4 * dx + dy], rwy.at[4 * dx + dy], w, 2 * ((y + dy) % Y) + c)

    def wo_yr(dx, i):
        ref = wo.at[narrow_at(1 + 2 * i), half_rows(dx, i)]
        return remote(ref, ref, swy.at[4 * dx + 2 * i], rwy.at[4 * dx + 2 * i], w, 2 * ((y + 1 + 2 * i) % Y) + c)

    def wo_p(dx, dy):
        ref = wo.at[narrow_at(dy), wo_rows(dx)]
        return remote(ref, ref, swp.at[4 * dx + dy], rwp.at[4 * dx + dy], w, n + up)

    def wo_on(dx):
        wo_y(dx, 1).start()
        wo_y(dx, 3).start()
        wo_p(dx, 0).start()

    def wo_relay(dx):
        for i in range(2):
            arrived(wo.at[narrow_at(1 + 2 * i), wo_rows(dx)], rwy.at[4 * dx + 1 + 2 * i])
            wo_yr(dx, i).start()
            wo_p(dx, 1 + 2 * i).start()

    def wo_last(dx):
        for i in range(2):
            arrived(wo.at[narrow_at(2), half_rows(dx, i)], rwy.at[4 * dx + 2 * i])
        wo_p(dx, 2).start()

    owner_row = own_ref[...]
    owner_col = jnp.broadcast_to(owner_row.astype(f32), (128, 128)).T
    same = (owner_col == owner_row.astype(f32)) & (iota((128, 128), 0) < iota((128, 128), 1))
    rank = jnp.sum(same.astype(f32), axis=0, keepdims=True)
    slot_of = owner_row * 8 + rank.astype(i32)
    picker = (iota((256, 128), 0) == slot_of).astype(bf16)

    pl.semaphore_wait(barrier, X * NN - 1 + NW - X)

    rows_x = pl.ds(pl.multiple_of(32 * x, 32), 32)
    rows_q = pl.ds(pl.multiple_of(16 * x, 16), 16)
    main, tail = pl.ds(0, D), pl.ds(D, 128)
    starts = []
    for i in range(2):
        dw = (2 * c + i) * Z + z
        starts.append((k_ref.at[i], kv.at[0, z, rows_x, main], s0.at[i], r_kv.at[x], dw, 2 * y))
        starts.append((v_ref.at[i], kv.at[1, z, rows_x, main], s0.at[2 + i], r_kv.at[x], dw, 2 * y + 1))
    for i in range(2):
        dw = (2 * c + i) * Z + z
        for d in range(2):
            starts.append((q_ref.at[i, pl.ds(16 * d, 16)], qb.at[rows_q], s0.at[4 + 2 * i + d], r_q.at[x], dw,
                           2 * y + d))
    for dx in range(X):
        starts.append((oh, kv.at[c, z, rows_x, tail], s0.at[8 + dx], r_oh.at[x], dx * Z + z, n))
    for args in starts:
        send(*args)

    @pl.loop(1, Z)
    def _(d):
        wo_z(d).start()

    m_s[...] = jnp.full_like(m_s, -3e38)
    acc_s[...] = jnp.zeros_like(acc_s)

    lane = iota((128, 128), 1)
    ones_col = (lane == HD).astype(bf16)

    def piece(ref_slice, j):
        t, r = (HD * j) // 128, (HD * j) % 128
        out = ref_slice(t)
        if r:
            out = pltpu.roll(out, 128 - r, 1)
        if r + HD > 128:
            nxt = pltpu.roll(ref_slice(t + 1), 128 - r, 1)
            out = jnp.where(iota(out.shape, 1) < 128 - r, out, nxt)
        return out

    def attend(slot):
        ohs = kv[0, slot, :, D:D + 128]
        for jj in range(4):
            ohr = pltpu.roll(ohs, (HD - 32 * jj) % 128, 1)
            for j in range(4 * jj, 4 * jj + 4):
                kj = piece(lambda t: kv[0, slot, :, 128 * t:128 * t + 128], j)
                kx[128 * j:128 * j + 128, :] = jnp.where(lane < HD, kj, ohr)
                vj = piece(lambda t: kv[1, slot, :, 128 * t:128 * t + 128], j)
                vx[128 * j:128 * j + 128, :] = jnp.where(lane < HD, vj, ones_col)

        def scores(qt):
            return lax.dot_general(qx[256 * qt:256 * qt + 256, :], kx[...], (((1,), (1,)), ((), ())),
                                   preferred_element_type=f32)

        s = scores(0)
        for qt in range(X):
            s_next = scores(qt + 1) if qt + 1 < X else None
            rows = slice(256 * qt, 256 * qt + 256)
            m_old = m_s[rows, :]
            m_new = jnp.maximum(m_old, jnp.max(s, axis=1, keepdims=True))
            p = jnp.exp2((s - m_new) * scale).astype(bf16)
            fix = jnp.exp2((m_old - m_new) * scale)
            acc_s[rows, :] = acc_s[rows, :] * fix + jnp.dot(p, vx[...], preferred_element_type=f32)
            m_s[rows, :] = m_new
            s = s_next

    for i in range(X):
        arrived(kv.at[c, z, pl.ds(32 * i, 32), main], r_kv.at[i])
        arrived(kv.at[c, z, pl.ds(32 * i, 32), tail], r_oh.at[i])

    def to_partner(slot):
        return remote(kv.at[c, slot], kv.at[c, slot], dss.at[slot], drs.at[slot], w, n + up)

    def onward(k, t):
        slot = slot_at(k)
        step = jnp.where(t % 2 == 1, up, -up)
        dz = (z + step + Z) % Z
        return remote(kv.at[c, slot], kv.at[c, slot], ss.at[t], rs.at[t], x * Z + dz, n)

    onward(0, 1).start()
    onward(0, 2).start()
    to_partner(z).start()

    wm_z(0, 1).start()
    wm_z(0, 2).start()

    for i in range(X):
        arrived(qb.at[pl.ds(16 * i, 16)], r_q.at[i])
    lane16 = iota((16, 128), 1)
    for i in range(X):
        ohq = kv[c, z, pl.ds(pl.multiple_of(32 * i + 16 * c, 16), 16), D:D + 128]
        for jj in range(4):
            ohr = (pltpu.roll(ohq, (HD - 32 * jj) % 128, 1) - bf16(1)) * bf16(BIG)
            ohr = jnp.where(lane16 < HD + 16, ohr, bf16(0))
            for j in range(4 * jj, 4 * jj + 4):
                qj = piece(lambda t: qb[16 * i:16 * i + 16, 128 * t:128 * t + 128], j)
                qx[256 * i + 16 * j:256 * i + 16 * j + 16, :] = jnp.where(lane16 < HD, qj, ohr)

    @pl.loop(1, Z)
    def _(d):
        arrived(wo.at[n, x * Z + (z - d + Z) % Z], rwz.at[d])
    for dx in (1, 3):
        wo_x(dx).start()
        wm_x(0, dx).start()
    wo_on(0)

    @pl.loop(0, Z)
    def _(k):
        def take(kk):
            slot = slot_at(kk)
            arrived(kv.at[c, slot], rs.at[kk])

            @pl.when(kk + 2 < Z)
            def _():
                onward(kk, kk + 2).start()
            to_partner(slot).start()

        @pl.when(k % 2 == 1)
        def _():
            take(k)

            @pl.when(k + 1 < Z)
            def _():
                take(k + 1)
        slot = slot_at(k)
        arrived(kv.at[1 - c, slot], drs.at[slot])
        attend(slot)

        @pl.when(k >= 1)
        def _():
            arrived(wm_at(k, 0), rmz.at[k])

            @pl.when(k + 2 < Z)
            def _():
                wm_z(k, k + 2).start()
            for dx in (1, 3):
                wm_x(k, dx).start()

        @pl.when(k == 1)
        def _():
            for i in range(2):
                arrived(wo.at[n, wo_rows(1 + 2 * i)], rwx.at[1 + 2 * i])
                wo_xr(i).start()

        @pl.when(k == 3)
        def _():
            for i in range(2):
                arrived(wo.at[n, half_rows(2, i)], rwx.at[2 * i])

        def nth(i):
            return i + jnp.where(i == 2, 1, 0) - jnp.where(i == 3, 1, 0)

        @pl.when((k >= 1) & (k < X))
        def _():
            wo_on(nth(k))

        @pl.when((k >= 1) & (k < X + 1))
        def _():
            wo_relay(nth(k - 1))

        @pl.when((k >= 2) & (k < X + 2))
        def _():
            wo_last(nth(k - 2))

        @pl.when(k >= 1)
        def _():
            wm_relay(k - 1)

    i0, i1 = iota((256, 256), 0), iota((256, 256), 1)
    grp, pos = i0 & 15, (i0 >> 4) & 3
    r_src = 4 * (i0 >> 6) + (grp >> 2)
    j_src = 4 * (grp & 3) + pos
    perm256 = (i1 == j_src * 16 + r_src).astype(bf16)
    lane256 = iota((256, 128), 1)
    for i in range(X):
        a = acc_s[256 * i:256 * i + 256, :]
        a = jnp.where(lane256 < HD, a / a[:, HD:HD + 1], 0.0).astype(bf16)
        ob[4 * i:4 * i + 4] = jnp.dot(perm256, a, preferred_element_type=f32).astype(bf16).reshape(4, 64, 128)
    head = 4 * y + x
    for i in range(X):
        for l in range(4):
            send(ob.at[4 * i + l], orecv.at[head], so.at[4 * i + l], ro.at[head], i * Z + z, 4 * c + l)

    wm_relay(Z - 1)

    @pl.loop(0, X)
    def _(dx):
        for dy in range(Y):
            arrived(wo.at[2 * ((y - dy + Y) % Y) + 1 - c, wo_rows(dx)], rwp.at[4 * dx + dy])
    hid = jnp.zeros((64, TILE), f32)
    for i in range(NN):
        arrived(orecv.at[2 * i], ro.at[2 * i])
        arrived(orecv.at[2 * i + 1], ro.at[2 * i + 1])
        a = jnp.concatenate([orecv[2 * i], orecv[2 * i + 1]], axis=1)
        hid = hid + lax.dot_general(a, wo[i].reshape(TILE, 256), (((1,), (1,)), ((), ())),
                                    preferred_element_type=f32)
    a256, b256 = iota((256, 256), 0), iota((256, 256), 1)
    narrowed = ((b256 == 52 * (a256 >> 6) + (a256 & 63)) & ((a256 & 63) < 52)).astype(bf16)
    for i in range(NN):
        h = (res[:, 256 * i:256 * i + 256].astype(f32) + hid[:, 256 * i:256 * i + 256]).astype(bf16)
        hb[i] = jnp.dot(h, narrowed, preferred_element_type=f32).astype(bf16)
    for i in range(NN):
        send(hb.at[i], hrecv.at[n], sh.at[i], rh.at[n], w, i)
    whole = jnp.concatenate([hb[i][:, 0:208] for i in range(NN)], axis=1)
    back = (g64 == 4 * (p64 & 15) + (p64 >> 4)).astype(bf16)
    hout_ref[...] = jnp.dot(back, whole, preferred_element_type=f32).astype(bf16)

    for i in range(NN):
        arrived(hrecv.at[i], rh.at[i])
    @pl.loop(0, Z)
    def _(k):
        for i in range(2):
            arrived(wm_half(k, 2, i), rmx.at[4 * k + 2 * i])
    part = jnp.zeros((128, TILE), f32)
    for j in range(4):
        part = part + lax.dot_general(hrecv[:, 16 * j:16 * j + 16, :].reshape(128, 256),
                                      wm[:, j].reshape(TILE, 256), (((1,), (1,)), ((), ())),
                                      preferred_element_type=f32)
    for i in range(NN):
        fb[i] = part[:, 256 * i:256 * i + 256].astype(bf16)
    for i in range(NN):
        send(fb.at[i], frecv.at[n], sf.at[i], rf.at[n], w, i)
    feat = jnp.zeros((128, 256), f32)
    for i in range(NN):
        arrived(frecv.at[i], rf.at[i])
        feat = feat + frecv[i].astype(f32)

    feat = jnp.dot(feat.astype(bf16), narrowed, preferred_element_type=f32)
    outg[...] = jnp.dot(picker, feat.astype(bf16), preferred_element_type=f32).reshape(NW, 8, 256).astype(bf16)

    @pl.loop(0, NW)
    def _(i):
        send(outg.at[i], drecv.at[w], sd.at[i], rd.at[w], i, n)

    @pl.loop(0, NW)
    def _(i):
        arrived(drecv.at[i], rd.at[i])
    dout_ref[...] = drecv[...].astype(f32).reshape(256, 256).astype(bf16)[:, 0:208]

    for src, dst, ssem, rsem, dw, dn in starts:
        sent(src, ssem, dw, dn)

    @pl.loop(1, Z)
    def _(t):
        onward(jnp.maximum(t - 2, 0), t).wait_send()
        wo_z(t).wait_send()
        wm_z(jnp.maximum(t - 2, 0), t).wait_send()
    for i in range(2):
        wo_x(1 + 2 * i).wait_send()
        wo_xr(i).wait_send()

    @pl.loop(0, Z)
    def _(k):
        for i in range(2):
            wm_x(k, 1 + 2 * i).wait_send()
            wm_xr(k, i).wait_send()

    @pl.loop(0, X)
    def _(dx):
        for i in range(2):
            wo_y(dx, 1 + 2 * i).wait_send()
            wo_yr(dx, i).wait_send()
        for dy in range(Y):
            wo_p(dx, dy).wait_send()

    @pl.loop(0, Z)
    def _(t):
        to_partner(t).wait_send()
    for i in range(X):
        for l in range(4):
            sent(ob.at[4 * i + l], so.at[4 * i + l], i * Z + z, 4 * c + l)
    for i in range(NN):
        sent(hb.at[i], sh.at[i], w, i)
        sent(fb.at[i], sf.at[i], w, i)

    @pl.loop(0, NW)
    def _(i):
        sent(outg.at[i], sd.at[i], i, n)


def shards(hidden_in, queries, keys, values, out_weight, merge_weight, segment_ids, owners):
    vm = pl.BlockSpec(memory_space=pltpu.VMEM)
    dma = pltpu.SemaphoreType.DMA
    return pl.pallas_call(
        kernel,
        out_shape=(jax.ShapeDtypeStruct((64, D), bf16), jax.ShapeDtypeStruct((256, 208), bf16)),
        in_specs=[vm] * 8,
        out_specs=(vm, vm),
        scratch_shapes=[
            pltpu.VMEM((2, Z, 128, D + 128), bf16),
            pltpu.VMEM((64, D), bf16),
            pltpu.VMEM((32, 128), bf16),
            pltpu.VMEM((128, 128), f32),
            pltpu.VMEM((2048, 128), bf16),
            pltpu.VMEM((2048, 128), bf16),
            pltpu.VMEM((1024, 128), bf16),
            pltpu.VMEM((1024, 1), f32),
            pltpu.VMEM((1024, 128), f32),
            pltpu.VMEM((16, 64, 128), bf16),
            pltpu.VMEM((16, 64, 128), bf16),
            pltpu.VMEM((NN, 64, 256), bf16),
            pltpu.VMEM((NN, 64, 256), bf16),
            pltpu.VMEM((NN, 128, 256), bf16),
            pltpu.VMEM((NN, 128, 256), bf16),
            pltpu.VMEM((NW, 8, 256), bf16),
            pltpu.VMEM((NW, 8, 256), bf16),
            pltpu.VMEM((64, TILE), bf16),
            pltpu.VMEM((NN, NW, 64, 256), bf16),
            pltpu.VMEM((NW, 4, 64, 256), bf16),
            dma((12,)), dma((X,)), dma((X,)), dma((X,)),
            dma((Z,)), dma((Z,)), dma((Z,)), dma((Z,)),
            dma((16,)), dma((16,)), dma((NN,)), dma((NN,)), dma((NN,)), dma((NN,)),
            dma((NW,)), dma((NW,)),
            dma((Z,)), dma((Z,)), dma((Z,)), dma((Z,)), dma((X,)), dma((X,)), dma((4 * Z,)), dma((4 * Z,)),
            dma((16,)), dma((16,)), dma((16,)), dma((16,)),
        ],
        compiler_params=pltpu.CompilerParams(collective_id=0, has_side_effects=True,
                                             vmem_limit_bytes=60 * 1024 * 1024),
    )(queries, keys, values, segment_ids.reshape(1, 128), owners.reshape(1, 128), hidden_in, out_weight, merge_weight)


def solution(mesh):
    return jax.shard_map(
        shards,
        mesh=mesh,
        in_specs=(
            P(("wide", "narrow"), None),
            P("narrow", "wide", None),
            P("narrow", "wide", None),
            P("narrow", "wide", None),
            P("narrow", "wide"),
            P(None, "narrow", "wide"),
            P("wide"),
            P("wide", None),
        ),
        out_specs=(P(("wide", "narrow"), None), P("wide", "narrow")),
        check_vma=False,
    )
```
